32 devices in a mesh: tm: 8 (over y, x, core), rows: 4 (over z).
Axes of the slice: x: 2, y: 2, z: 4, core: 2. Of those that a mesh axis runs over, the one named last changes fastest.
Arguments:
- frames_in: bfloat16 [32, 32, 32, 512], P('tm', 'rows'), may hold values from -6 to 6
- weight_in: bfloat16 [2, 512, 4608], P(None, 'rows'), may hold values from -0.09375 to 0.09375
- weight_out: bfloat16 [9, 2, 512, 512], P(None, None, 'rows'), may hold values from -0.015625 to 0.015625
- log_decay: float32 [512], replicated, may hold values from 0.0003125 to 0.06
- rotation: float32 [512], replicated, may hold values from -3.140625 to 3.140625
- start_state: float32 [32, 32, 2, 512], P('rows'), may hold values from -12 to 12
- skip_gain: float32 [512], replicated, may hold values from -1 to 1
Outputs:
- frames_out: bfloat16 [32, 32, 32, 512], P('tm', 'rows')
The draws below stay inside these ranges and needn't reach their ends.
All inputs are finite; a program needn't handle non-finite values.
Results may differ from the reference program's by a relative error of at most 0.0047.
Values may be sent and summed in bfloat16 or wider, within the bound.
A program may use at most 128 MiB of HBM per device.

```python
import math
import jax
import jax.numpy as jnp
from jax import lax

D = 512
P_SIZE = 512
HH = 32
WW = 32
FRAMES = 32


def levels(stream_key, shape, pieces, smallest, largest):
    level, own = 1.0, jax.random.fold_in(stream_key, 6)
    for axis_at, blocks in pieces:
        steps = jnp.exp(jax.random.uniform(jax.random.fold_in(own, axis_at), (blocks,), jnp.float32, smallest / len(pieces), largest / len(pieces)))
        level = level * jnp.repeat(steps, shape[axis_at] // blocks).reshape([-1 if axis == axis_at else 1 for axis in range(len(shape))])
    return level


def noise(own_key, extent, scale, bound, pieces=(), dtype=jnp.bfloat16):
    gain = levels(own_key, extent, pieces, -0.22, 0.18) if pieces else 1.0
    array = jax.random.normal(own_key, extent, jnp.float32) * scale * gain
    return jnp.minimum(jnp.maximum(array, -bound), bound).astype(dtype)


def setup_inputs(seed: int = 0) -> dict:
    arg_keys = jax.random.split(jax.random.key(seed), 8)
    frames_in = noise(arg_keys[0], (FRAMES, HH, WW, D), 1.0, 6.0, ((0, 8), (1, 4)))
    weight_in = noise(arg_keys[1], (2, P_SIZE, 9 * D), (9 * D) ** -0.5, 0.09375, ((1, 4),))
    weight_out = noise(arg_keys[2], (9, 2, P_SIZE, D), (16 * 18 * P_SIZE) ** -0.5, 0.015625, ((2, 4),))
    log_decay = jnp.clip(jnp.exp(jax.random.uniform(arg_keys[3], (P_SIZE,), jnp.float32, math.log(0.0003125), math.log(0.06))), 0.0003125, 0.06)
    rotation = jnp.clip(jax.random.uniform(arg_keys[4], (P_SIZE,), jnp.float32, -3.140625, 3.140625), -3.140625, 3.140625)
    start_state = noise(arg_keys[5], (HH, WW, 2, P_SIZE), 2.0, 12.0, ((0, 4),), jnp.float32)
    skip_gain = jnp.clip(jax.random.uniform(arg_keys[6], (D,), jnp.float32, -1.0, 1.0), -1.0, 1.0)
    return {"frames_in": frames_in, "weight_in": weight_in, "weight_out": weight_out, "log_decay": log_decay, "rotation": rotation, "start_state": start_state, "skip_gain": skip_gain}


def conv_same(field, weight, channels):
    height = field.shape[0]
    columns = field.shape[1]
    padded = jnp.pad(field, ((1, 1), (1, 1), (0, 0)))
    summed = jnp.zeros((height, columns, weight.shape[0]), jnp.float32)
    for tap_index in range(9):
        row_shift = tap_index // 3
        col_shift = tap_index % 3
        window = padded[row_shift:row_shift + height, col_shift:col_shift + columns, :]
        weight_tap = weight[:, tap_index * channels:(tap_index + 1) * channels]
        summed = summed + lax.dot_general(window, weight_tap, (((2,), (1,)), ((), ())), preferred_element_type=jnp.float32)
    return summed


def reference(frames_in, weight_in, weight_out, log_decay, rotation, start_state, skip_gain):
    modulus = jnp.exp(-log_decay)
    lam_re = modulus * jnp.cos(rotation)
    lam_im = modulus * jnp.sin(rotation)
    matrix_in = weight_in.reshape(2 * P_SIZE, 9 * D)
    matrix_out = weight_out.reshape(18 * P_SIZE, D).T
    driven = lax.map(lambda single: conv_same(single, matrix_in, D), frames_in)

    def advance(carried, forcing):
        state_re, state_im = carried
        new_re = lam_re * state_re - lam_im * state_im + forcing[..., :P_SIZE]
        new_im = lam_re * state_im + lam_im * state_re + forcing[..., P_SIZE:]
        return (new_re, new_im), jnp.concatenate([new_re, new_im], -1).astype(jnp.bfloat16)

    _, held = lax.scan(advance, (start_state[:, :, 0, :], start_state[:, :, 1, :]), driven)
    mixing = lax.map(lambda single: conv_same(single, matrix_out, 2 * P_SIZE), held)
    pre_act = mixing + skip_gain * frames_in.astype(jnp.float32)
    return jax.nn.gelu(pre_act, approximate=False).astype(jnp.bfloat16)
```

```python
import jax
import jax.numpy as jnp
from jax import lax
from jax.sharding import PartitionSpec as P


def passed_along(value, axis, steps):
    count = lax.axis_size(axis)
    first, last = (max(0, -steps), min(count, count - steps))
    return lax.ppermute(value, axis, [(source, source + steps) for source in range(first, last)])


def extended_2(cells, sides, width):
    for axis, dim in sides:
        count = lax.axis_size(axis)
        ends = count - 1
        head = lax.slice_in_dim(cells, 0, width, axis=dim)
        tail = lax.slice_in_dim(cells, cells.shape[dim] - width, cells.shape[dim], axis=dim)
        cells = jnp.concatenate(
            [
                lax.ppermute(tail, axis, [(i, (i + 1) % count) for i in range(ends)]),
                cells,
                lax.ppermute(head, axis, [((i + 1) % count, i) for i in range(ends)]),
            ],
            axis=dim,
        )
    return cells


def pad_field(field, rows_pad):
    widths = [(0, 0)] * field.ndim
    widths[1] = (rows_pad, rows_pad)
    widths[2] = (1, 1)
    return jnp.pad(field, widths)


def in_term(padded, piece, height, columns):
    parts, state_width, span = piece.shape
    channels = span // 9
    matrix = piece.reshape(parts * state_width, span)
    summed = jnp.zeros((padded.shape[0], height, columns, parts * state_width), jnp.float32)
    for tap_index in range(9):
        row_shift = tap_index // 3
        col_shift = tap_index % 3
        window = padded[:, row_shift : row_shift + height, col_shift : col_shift + columns, :]
        weight_tap = matrix[:, tap_index * channels : (tap_index + 1) * channels]
        summed = summed + lax.dot_general(
            window, weight_tap, (((3,), (1,)), ((), ())), preferred_element_type=jnp.float32
        )
    return summed.reshape(padded.shape[0], height, columns, parts, state_width)


def out_term(padded_held, piece, height, columns):
    summed = jnp.zeros((padded_held.shape[0], height, columns, piece.shape[3]), jnp.float32)
    for tap_index in range(9):
        row_shift = tap_index // 3
        col_shift = tap_index % 3
        window = padded_held[:, row_shift : row_shift + height, col_shift : col_shift + columns]
        summed = summed + lax.dot_general(
            window,
            piece[tap_index],
            (((3, 4), (0, 1)), ((), ())),
            preferred_element_type=jnp.float32,
        )
    return summed


def run_states(driven, start_re, start_im, log_rate, angle):
    frame_count = driven.shape[0]
    modulus = jnp.exp(-log_rate)
    lam_re = modulus * jnp.cos(angle)
    lam_im = modulus * jnp.sin(angle)
    is_first = lax.axis_index("tm") == 0
    begin_re = jnp.where(is_first, start_re, jnp.float32(0.0))
    begin_im = jnp.where(is_first, start_im, jnp.float32(0.0))

    def advance(carried, forcing):
        state_re, state_im = carried
        force_re, force_im = forcing
        new_re = lam_re * state_re - lam_im * state_im + force_re
        new_im = lam_re * state_im + lam_im * state_re + force_im
        return ((new_re, new_im), (new_re, new_im))

    (tail_re, tail_im), (local_re, local_im) = lax.scan(
        advance, (begin_re, begin_im), (driven[..., 0, :], driven[..., 1, :])
    )
    carry_re, carry_im = passed_along((tail_re, tail_im), "tm", 1)
    reach = 1
    while reach < lax.axis_size("tm"):
        far_re, far_im = passed_along((carry_re, carry_im), "tm", reach)
        jump_mod = jnp.exp(-log_rate * (frame_count * reach))
        jump_re = jump_mod * jnp.cos(angle * (frame_count * reach))
        jump_im = jump_mod * jnp.sin(angle * (frame_count * reach))
        carry_re, carry_im = (
            carry_re + jump_re * far_re - jump_im * far_im,
            carry_im + jump_re * far_im + jump_im * far_re,
        )
        reach *= 2
    step_count = jnp.arange(1, frame_count + 1, dtype=jnp.float32)[:, None, None, None]
    power_mod = jnp.exp(-log_rate * step_count)
    power_re = power_mod * jnp.cos(angle * step_count)
    power_im = power_mod * jnp.sin(angle * step_count)
    states_re = local_re + power_re * carry_re - power_im * carry_im
    states_im = local_im + power_re * carry_im + power_im * carry_re
    return jnp.stack([states_re, states_im], 3).astype(jnp.bfloat16)


def gathered(piece, axis):
    count = lax.axis_size("tm")
    width = piece.shape[axis] // count
    own = lax.dynamic_slice_in_dim(piece, lax.axis_index("tm") * width, width, axis)
    return lax.all_gather(own, ("rows", "tm"), axis=axis, tiled=True)


def on_device(frames_in, weight_in, weight_out, log_decay, rotation, start_state, skip_gain):
    frame_count, band_rows, columns, channels = frames_in.shape
    extended = extended_2(frames_in, (("rows", 1),), 1)
    padded = pad_field(extended, 0)
    driven = in_term(
        padded, gathered(weight_in, 1), band_rows, columns
    )
    held = run_states(driven, start_state[:, :, 0, :], start_state[:, :, 1, :], log_decay, rotation)
    held = extended_2(held, (("rows", 1),), 1)
    held_padded = pad_field(held, 0)
    mixing = out_term(
        held_padded, gathered(weight_out, 2), band_rows, columns
    )
    pre_act = mixing + skip_gain * frames_in.astype(jnp.float32)
    return jax.nn.gelu(pre_act, approximate=False).astype(jnp.bfloat16)


def solution(mesh):
    return jax.shard_map(
        on_device,
        mesh=mesh,
        in_specs=(
            P("tm", "rows", None, None),
            P(None, "rows", None),
            P(None, None, "rows", None),
            P(),
            P(),
            P("rows", None, None, None),
            P(),
        ),
        out_specs=P("tm", "rows", None, None),
        check_vma=False,
    )
```

```python
import jax
import jax.numpy as jnp
from jax import lax
from jax.sharding import Mesh, PartitionSpec as P

CHIPS, CORE, ROWS = "chips", "core", "rows"


def shifted(value, axis, step):
    count = lax.axis_size(axis)
    pairs = [(i, i + step) for i in range(count) if 0 <= i + step < count]
    return lax.ppermute(value, axis, pairs)


def swapped(value):
    return lax.ppermute(value, CORE, [(0, 1), (1, 0)])


def with_halo(field):
    above = shifted(field[:, -1:], ROWS, 1)
    below = shifted(field[:, :1], ROWS, -1)
    return jnp.concatenate([above, field, below], axis=1)


def gathered(piece, axis):
    return lax.all_gather(piece, (ROWS, CHIPS), axis=axis, tiled=True)


def conv(field, weight, form):
    return lax.conv_general_dilated(
        field, weight, (1, 1), ((0, 0), (1, 1)),
        dimension_numbers=("NHWC", form, "NHWC"),
        preferred_element_type=jnp.float32,
    )


def powers(log_rate, angle, exponent):
    modulus = jnp.exp(-log_rate * exponent)
    return modulus * jnp.cos(angle * exponent), modulus * jnp.sin(angle * exponent)


def on_device(frames_in, weight_in, weight_out, log_decay, rotation, start_state, skip_gain):
    frame_count, band_rows, columns, channels = frames_in.shape
    shard = weight_in.shape[1]
    chips, cores, rows = (lax.axis_size(a) for a in (CHIPS, CORE, ROWS))
    core, chip = lax.axis_index(CORE), lax.axis_index(CHIPS)
    half, width = shard // cores, shard // (cores * chips)
    at = core * half + chip * width

    def own(vector, axis):
        shape = vector.shape
        split = vector.reshape(shape[:axis] + (rows, cores, half) + shape[axis + 1 :])
        split = lax.dynamic_index_in_dim(split, core, axis + 1, keepdims=False)
        return split.reshape(shape[:axis] + (rows * half,) + shape[axis + 1 :])

    states = rows * half
    slice_in = lax.dynamic_slice_in_dim(weight_in, at, width, 1)
    slice_out = lax.dynamic_slice_in_dim(weight_out, at, width, 2)
    in_parts = [gathered(slice_in[part], 0) for part in range(2)]
    out_full = gathered(slice_out, 2)

    mine = with_halo(frames_in)
    theirs = swapped(mine)
    first = jnp.where(core == 0, mine, theirs)
    second = jnp.where(core == 0, theirs, mine)
    field = jnp.concatenate([first, second], axis=0)
    total = field.shape[0]

    driven = [
        conv(field, w.reshape(states, 3, 3, channels), "OHWI") for w in in_parts
    ]

    log_rate, angle = own(log_decay, 0), own(rotation, 0)
    start = own(start_state, 3)
    lam_re, lam_im = powers(log_rate, angle, jnp.float32(1.0))
    state_re = jnp.where(chip == 0, start[:, :, 0], jnp.float32(0.0))
    state_im = jnp.where(chip == 0, start[:, :, 1], jnp.float32(0.0))
    local = []
    for t in range(total):
        state_re, state_im = (
            lam_re * state_re - lam_im * state_im + driven[0][t],
            lam_re * state_im + lam_im * state_re + driven[1][t],
        )
        local.append((state_re, state_im))
    tail = jnp.stack([state_re, state_im]).astype(jnp.bfloat16)
    carry_re = carry_im = jnp.float32(0.0)
    for step in range(1, chips):
        far = shifted(tail, CHIPS, step).astype(jnp.float32)
        jump_re, jump_im = powers(log_rate, angle, jnp.float32(total * (step - 1)))
        carry_re = carry_re + jump_re * far[0] - jump_im * far[1]
        carry_im = carry_im + jump_re * far[1] + jump_im * far[0]
    held = []
    for t in range(total):
        pow_re, pow_im = powers(log_rate, angle, jnp.float32(t + 1))
        held.append(
            jnp.concatenate(
                [
                    local[t][0] + pow_re * carry_re - pow_im * carry_im,
                    local[t][1] + pow_re * carry_im + pow_im * carry_re,
                ],
                axis=-1,
            ).astype(jnp.bfloat16)
        )
    held = with_halo(jnp.stack(held))

    out_weight = out_full.reshape(3, 3, 2 * states, channels)
    held_theirs = lax.dynamic_slice_in_dim(held, (1 - core) * frame_count, frame_count, 0)
    held_mine = lax.dynamic_slice_in_dim(held, core * frame_count, frame_count, 0)
    sent = conv(held_theirs, out_weight, "HWIO").astype(jnp.bfloat16)
    got = swapped(sent).astype(jnp.float32)
    mixing = conv(held_mine, out_weight, "HWIO") + got
    pre_act = mixing + skip_gain * frames_in.astype(jnp.float32)
    return jax.nn.gelu(pre_act, approximate=False).astype(jnp.bfloat16)


def solution(mesh):
    count, rows = mesh.devices.shape
    fine = Mesh(mesh.devices.reshape(count // 2, 2, rows), (CHIPS, CORE, ROWS))
    frames = P((CHIPS, CORE), ROWS, None, None)
    return jax.shard_map(
        on_device,
        mesh=fine,
        in_specs=(
            frames,
            P(None, ROWS, None),
            P(None, None, ROWS, None),
            P(),
            P(),
            P(ROWS, None, None, None),
            P(),
        ),
        out_specs=frames,
        check_vma=False,
    )
```

```python
import functools
import jax
import jax.numpy as jnp
from jax import lax
from jax.experimental import pallas as pl
from jax.experimental.pallas import tpu as pltpu
from jax.sharding import Mesh, PartitionSpec as P

CHIPS, CORE, ROWS = "chips", "core", "rows"


def shifted(value, axis, step):
    count = lax.axis_size(axis)
    pairs = [(i, i + step) for i in range(count) if 0 <= i + step < count]
    return lax.ppermute(value, axis, pairs)


def swapped(value):
    return lax.ppermute(value, CORE, [(0, 1), (1, 0)])


def with_halo(field):
    above = shifted(field[:, -1:], ROWS, 1)
    below = shifted(field[:, :1], ROWS, -1)
    return jnp.concatenate([above, field, below], axis=1)


def chip_at(place, chips):
    far = place // (chips // 2)
    return (1 - far) * (2 * place) + far * (2 * (chips - 1 - place) + 1)


def place_of(chip, chips):
    odd = chip % 2
    return (1 - odd) * (chip // 2) + odd * (chips - 1 - chip // 2)


def spread_kernel(leads, chips, rows, own_ref, full_ref, z_send, z_recv, r_send, r_recv, own_sem):
    chip, row = lax.axis_index(CHIPS), lax.axis_index(ROWS)
    place = place_of(chip, chips)
    onward = chip_at((place + 1) % chips, chips)
    back = chip_at((place + chips - 1) % chips, chips)
    many = chips // 2

    barrier = pltpu.get_barrier_semaphore()

    def greet(**where):
        pl.semaphore_signal(
            barrier, inc=1, device_id=where, device_id_type=pl.DeviceIdType.MESH
        )

    greet(chips=onward)
    greet(chips=back)

    @pl.when(row > 0)
    def _():
        greet(rows=row - 1)

    @pl.when(row < rows - 1)
    def _():
        greet(rows=row + 1)

    sides = (row + rows - 1) // rows + (2 * rows - 2 - row) // rows
    pl.semaphore_wait(barrier, 2 + sides)

    lead = (slice(None),) * leads

    def own_slice():
        return own_ref.at[lead + (chip // many, chip % many)]

    def block(shard, source, piece=None):
        at = lead + (source // many, shard, source % many)
        return full_ref.at[at if piece is None else at + (piece,)]

    keep = pltpu.make_async_copy(
        own_ref, full_ref.at[lead + (slice(None), row)], own_sem
    )
    keep.start()

    def line(side, step):
        step_way = 1 - 2 * side
        shard = row - step_way * step
        src = own_slice() if step == 0 else block(shard, chip)
        return pltpu.make_async_remote_copy(
            src_ref=src,
            dst_ref=block(shard, chip),
            send_sem=z_send.at[side, step],
            recv_sem=z_recv.at[side, step],
            device_id={ROWS: row + step_way},
            device_id_type=pl.DeviceIdType.MESH,
        )

    def landed(side, step):
        shard = row - (1 - 2 * side) * (step + 1)
        here = block(shard, chip)
        return pltpu.make_async_remote_copy(
            src_ref=here,
            dst_ref=here,
            send_sem=z_send.at[side, step],
            recv_sem=z_recv.at[side, step],
            device_id={ROWS: row},
            device_id_type=pl.DeviceIdType.MESH,
        )

    def ring(side, step, way, turn):
        turn_way = 1 - 2 * way
        shard = row - (1 - 2 * side) * (step + 1)
        source = chip_at((place - turn_way * turn + chips) % chips, chips)
        here = block(shard, source, way)
        return pltpu.make_async_remote_copy(
            src_ref=here,
            dst_ref=here,
            send_sem=r_send.at[side, step, way, turn],
            recv_sem=r_recv.at[side, step, way, turn],
            device_id={CHIPS: back if way else onward},
            device_id_type=pl.DeviceIdType.MESH,
        )

    def ring_landed(side, step, way, turn):
        turn_way = 1 - 2 * way
        shard = row - (1 - 2 * side) * (step + 1)
        source = chip_at((place - turn_way * (turn + 1) + 2 * chips) % chips, chips)
        here = block(shard, source, way)
        return pltpu.make_async_remote_copy(
            src_ref=here,
            dst_ref=here,
            send_sem=r_send.at[side, step, way, turn],
            recv_sem=r_recv.at[side, step, way, turn],
            device_id={CHIPS: back if way else onward},
            device_id_type=pl.DeviceIdType.MESH,
        )

    def sends(side, step):
        near = row - step if side == 0 else rows - 1 - row - step
        room = rows - 1 - row if side == 0 else row
        return jnp.logical_and(near >= 0, room > 0)

    def comes(side, step):
        return (row if side == 0 else rows - 1 - row) > step

    for side in range(2):

        @pl.when(sends(side, 0))
        def _():
            line(side, 0).start()

    for tick in range(rows - 1 + chips - 1):
        if tick < rows - 1:
            for side in range(2):

                @pl.when(comes(side, tick))
                def _():
                    landed(side, tick).wait_recv()
                    if tick + 1 < rows - 1:

                        @pl.when(sends(side, tick + 1))
                        def _():
                            line(side, tick + 1).start()

                    for way in range(2):
                        ring(side, tick, way, 0).start()

        for turn in range(1, chips):
            step = tick - turn
            if 0 <= step < rows - 1:
                for side in range(2):

                    @pl.when(comes(side, step))
                    def _():
                        for way in range(2):
                            ring_landed(side, step, way, turn - 1).wait_recv()
                            if turn < chips - 1:
                                ring(side, step, way, turn).start()

    for side in range(2):
        for step in range(rows - 1):

            @pl.when(sends(side, step))
            def _():
                line(side, step).wait_send()

            @pl.when(comes(side, step))
            def _():
                for way in range(2):
                    for turn in range(chips - 1):
                        ring(side, step, way, turn).wait_send()

    keep.wait()


def spread(own, leads, chips, rows, number):
    shape = own.shape[: leads + 1] + (rows,) + own.shape[leads + 1 :]
    any_space = pl.BlockSpec(memory_space=pl.ANY)
    return pl.pallas_call(
        functools.partial(spread_kernel, leads, chips, rows),
        out_shape=jax.ShapeDtypeStruct(shape, own.dtype),
        in_specs=[pl.BlockSpec(memory_space=pltpu.VMEM)],
        out_specs=any_space,
        scratch_shapes=[
            pltpu.SemaphoreType.DMA((2, rows - 1)),
            pltpu.SemaphoreType.DMA((2, rows - 1)),
            pltpu.SemaphoreType.DMA((2, rows - 1, 2, chips - 1)),
            pltpu.SemaphoreType.DMA((2, rows - 1, 2, chips - 1)),
            pltpu.SemaphoreType.DMA,
        ],
        compiler_params=pltpu.CompilerParams(collective_id=number, has_side_effects=True),
    )(own)


def conv(field, weight, form):
    return lax.conv_general_dilated(
        field, weight, (1, 1), ((0, 0), (1, 1)),
        dimension_numbers=("NHWC", form, "NHWC"),
        preferred_element_type=jnp.float32,
    )


def powers(log_rate, angle, exponent):
    modulus = jnp.exp(-log_rate * exponent)
    return modulus * jnp.cos(angle * exponent), modulus * jnp.sin(angle * exponent)


def on_device(frames_in, weight_in, weight_out, log_decay, rotation, start_state, skip_gain):
    frame_count, band_rows, columns, channels = frames_in.shape
    shard = weight_in.shape[1]
    chips, cores, rows = (lax.axis_size(a) for a in (CHIPS, CORE, ROWS))
    core, chip = lax.axis_index(CORE), lax.axis_index(CHIPS)
    half = shard // cores
    many = chips // 2
    piece = half // (2 * many)

    def own(vector, axis):
        shape = vector.shape
        split = vector.reshape(shape[:axis] + (rows, cores, half) + shape[axis + 1 :])
        split = lax.dynamic_index_in_dim(split, core, axis + 1, keepdims=False)
        return split.reshape(shape[:axis] + (rows * half,) + shape[axis + 1 :])

    states = rows * half
    slice_in = lax.dynamic_slice_in_dim(weight_in, core * half, half, 1)
    slice_out = lax.dynamic_slice_in_dim(weight_out, core * half, half, 2)
    in_full = spread(
        slice_in.reshape(2, many, 2, piece, 9 * channels), 0, chips, rows, 0
    ).reshape(2, states, 9 * channels)
    out_full = spread(
        slice_out.reshape(9, 2, many, 2, piece, channels), 1, chips, rows, 1
    )

    mine = with_halo(frames_in)
    theirs = swapped(mine)
    first = jnp.where(core == 0, mine, theirs)
    second = jnp.where(core == 0, theirs, mine)
    field = jnp.concatenate([first, second], axis=0)
    total = field.shape[0]

    driven = [
        conv(field, in_full[part].reshape(states, 3, 3, channels), "OHWI")
        for part in range(2)
    ]

    log_rate, angle = own(log_decay, 0), own(rotation, 0)
    start = own(start_state, 3)
    lam_re, lam_im = powers(log_rate, angle, jnp.float32(1.0))
    state_re = jnp.where(chip == 0, start[:, :, 0], jnp.float32(0.0))
    state_im = jnp.where(chip == 0, start[:, :, 1], jnp.float32(0.0))
    local = []
    for t in range(total):
        state_re, state_im = (
            lam_re * state_re - lam_im * state_im + driven[0][t],
            lam_re * state_im + lam_im * state_re + driven[1][t],
        )
        local.append((state_re, state_im))
    tail = jnp.stack([state_re, state_im]).astype(jnp.bfloat16)
    carry_re = carry_im = jnp.float32(0.0)
    for step in range(1, chips):
        far = shifted(tail, CHIPS, step).astype(jnp.float32)
        jump_re, jump_im = powers(log_rate, angle, jnp.float32(total * (step - 1)))
        carry_re = carry_re + jump_re * far[0] - jump_im * far[1]
        carry_im = carry_im + jump_re * far[1] + jump_im * far[0]
    held = []
    for t in range(total):
        pow_re, pow_im = powers(log_rate, angle, jnp.float32(t + 1))
        held.append(
            jnp.concatenate(
                [
                    local[t][0] + pow_re * carry_re - pow_im * carry_im,
                    local[t][1] + pow_re * carry_im + pow_im * carry_re,
                ],
                axis=-1,
            ).astype(jnp.bfloat16)
        )
    held = with_halo(jnp.stack(held))

    out_weight = out_full.reshape(3, 3, 2 * states, channels)
    held_theirs = lax.dynamic_slice_in_dim(held, (1 - core) * frame_count, frame_count, 0)
    held_mine = lax.dynamic_slice_in_dim(held, core * frame_count, frame_count, 0)
    sent = conv(held_theirs, out_weight, "HWIO").astype(jnp.bfloat16)
    got = swapped(sent).astype(jnp.float32)
    mixing = conv(held_mine, out_weight, "HWIO") + got
    pre_act = mixing + skip_gain * frames_in.astype(jnp.float32)
    return jax.nn.gelu(pre_act, approximate=False).astype(jnp.bfloat16)


def solution(mesh):
    count, rows = mesh.devices.shape
    fine = Mesh(mesh.devices.reshape(count // 2, 2, rows), (CHIPS, CORE, ROWS))
    frames = P((CHIPS, CORE), ROWS, None, None)
    return jax.shard_map(
        on_device,
        mesh=fine,
        in_specs=(
            frames,
            P(None, ROWS, None),
            P(None, None, ROWS, None),
            P(),
            P(),
            P(ROWS, None, None, None),
            P(),
        ),
        out_specs=frames,
        check_vma=False,
    )
```

```python
import functools
import jax
import jax.numpy as jnp
from jax import lax
from jax.experimental import pallas as pl
from jax.experimental.pallas import tpu as pltpu
from jax.sharding import Mesh, PartitionSpec as P

CHIPS, CORE, ROWS = "chips", "core", "rows"


def shifted(value, axis, step):
    count = lax.axis_size(axis)
    pairs = [(i, i + step) for i in range(count) if 0 <= i + step < count]
    return lax.ppermute(value, axis, pairs)


def swapped(value):
    return lax.ppermute(value, CORE, [(0, 1), (1, 0)])


def with_halo(field):
    above = shifted(field[:, -1:], ROWS, 1)
    below = shifted(field[:, :1], ROWS, -1)
    return jnp.concatenate([above, field, below], axis=1)


def chip_at(place, chips):
    far = place // (chips // 2)
    return (1 - far) * (2 * place) + far * (2 * (chips - 1 - place) + 1)


def place_of(chip, chips):
    odd = chip % 2
    return (1 - odd) * (chip // 2) + odd * (chips - 1 - chip // 2)


def meet(chips, rows, chip, row, onward, back):
    barrier = pltpu.get_barrier_semaphore()

    def greet(**where):
        pl.semaphore_signal(
            barrier, inc=1, device_id=where, device_id_type=pl.DeviceIdType.MESH
        )

    greet(chips=onward)
    greet(chips=back)

    @pl.when(row > 0)
    def _():
        greet(rows=row - 1)

    @pl.when(row < rows - 1)
    def _():
        greet(rows=row + 1)

    sides = (row + rows - 1) // rows + (2 * rows - 2 - row) // rows
    pl.semaphore_wait(barrier, 2 + sides)


def spreader(leads, chips, rows, own_ref, full_ref, z_send, z_recv, r_send, r_recv, own_sem):
    chip, row = lax.axis_index(CHIPS), lax.axis_index(ROWS)
    place = place_of(chip, chips)
    onward = chip_at((place + 1) % chips, chips)
    back = chip_at((place + chips - 1) % chips, chips)
    many = chips // 2
    lead = (slice(None),) * leads

    def own_slice():
        return own_ref.at[lead + (chip // many, chip % many)]

    def block(shard, source, piece=None):
        at = lead + (source // many, shard, source % many)
        return full_ref.at[at if piece is None else at + (piece,)]

    keep = pltpu.make_async_copy(
        own_ref, full_ref.at[lead + (slice(None), row)], own_sem
    )

    def line(side, step):
        step_way = 1 - 2 * side
        shard = row - step_way * step
        src = own_slice() if step == 0 else block(shard, chip)
        return pltpu.make_async_remote_copy(
            src_ref=src,
            dst_ref=block(shard, chip),
            send_sem=z_send.at[side, step],
            recv_sem=z_recv.at[side, step],
            device_id={ROWS: row + step_way},
            device_id_type=pl.DeviceIdType.MESH,
        )

    def landed(side, step):
        shard = row - (1 - 2 * side) * (step + 1)
        here = block(shard, chip)
        return pltpu.make_async_remote_copy(
            src_ref=here,
            dst_ref=here,
            send_sem=z_send.at[side, step],
            recv_sem=z_recv.at[side, step],
            device_id={ROWS: row},
            device_id_type=pl.DeviceIdType.MESH,
        )

    def ring(side, step, way, turn):
        turn_way = 1 - 2 * way
        shard = row - (1 - 2 * side) * (step + 1)
        source = chip_at((place - turn_way * turn + chips) % chips, chips)
        here = block(shard, source, way)
        return pltpu.make_async_remote_copy(
            src_ref=here,
            dst_ref=here,
            send_sem=r_send.at[side, step, way, turn],
            recv_sem=r_recv.at[side, step, way, turn],
            device_id={CHIPS: back if way else onward},
            device_id_type=pl.DeviceIdType.MESH,
        )

    def ring_landed(side, step, way, turn):
        turn_way = 1 - 2 * way
        shard = row - (1 - 2 * side) * (step + 1)
        source = chip_at((place - turn_way * (turn + 1) + 2 * chips) % chips, chips)
        here = block(shard, source, way)
        return pltpu.make_async_remote_copy(
            src_ref=here,
            dst_ref=here,
            send_sem=r_send.at[side, step, way, turn],
            recv_sem=r_recv.at[side, step, way, turn],
            device_id={CHIPS: back if way else onward},
            device_id_type=pl.DeviceIdType.MESH,
        )

    def sends(side, step):
        near = row - step if side == 0 else rows - 1 - row - step
        room = rows - 1 - row if side == 0 else row
        return jnp.logical_and(near >= 0, room > 0)

    def comes(side, step):
        return (row if side == 0 else rows - 1 - row) > step

    def begin():
        keep.start()
        for side in range(2):

            @pl.when(sends(side, 0))
            def _():
                line(side, 0).start()

    def advance(tick):
        if tick < rows - 1:
            for side in range(2):

                @pl.when(comes(side, tick))
                def _():
                    landed(side, tick).wait_recv()
                    if tick + 1 < rows - 1:

                        @pl.when(sends(side, tick + 1))
                        def _():
                            line(side, tick + 1).start()

                    for way in range(2):
                        ring(side, tick, way, 0).start()

        for turn in range(1, chips):
            step = tick - turn
            if 0 <= step < rows - 1:
                for side in range(2):

                    @pl.when(comes(side, step))
                    def _():
                        for way in range(2):
                            ring_landed(side, step, way, turn - 1).wait_recv()
                            if turn < chips - 1:
                                ring(side, step, way, turn).start()

    def finish():
        for side in range(2):
            for step in range(rows - 1):

                @pl.when(sends(side, step))
                def _():
                    line(side, step).wait_send()

                @pl.when(comes(side, step))
                def _():
                    for way in range(2):
                        for turn in range(chips - 1):
                            ring(side, step, way, turn).wait_send()

    return begin, advance, finish, keep


def spread_kernel(leads, chips, rows, *refs):
    chip, row = lax.axis_index(CHIPS), lax.axis_index(ROWS)
    place = place_of(chip, chips)
    onward = chip_at((place + 1) % chips, chips)
    back = chip_at((place + chips - 1) % chips, chips)
    meet(chips, rows, chip, row, onward, back)
    begin, advance, finish, keep = spreader(leads, chips, rows, *refs)
    begin()
    for tick in range(rows - 1 + chips - 1):
        advance(tick)
    finish()
    keep.wait()


def semaphores(chips, rows):
    return [
        pltpu.SemaphoreType.DMA((2, rows - 1)),
        pltpu.SemaphoreType.DMA((2, rows - 1)),
        pltpu.SemaphoreType.DMA((2, rows - 1, 2, chips - 1)),
        pltpu.SemaphoreType.DMA((2, rows - 1, 2, chips - 1)),
        pltpu.SemaphoreType.DMA,
    ]


GROUPS = 4


def drive_kernel(chips, rows, in_ref, out_ref, field_ref, driven_ref, full_out, full_in, *sems):
    chip, row = lax.axis_index(CHIPS), lax.axis_index(ROWS)
    place = place_of(chip, chips)
    onward = chip_at((place + 1) % chips, chips)
    back = chip_at((place + chips - 1) % chips, chips)
    meet(chips, rows, chip, row, onward, back)
    count = len(sems) // 2
    first = spreader(0, chips, rows, in_ref, full_in, *sems[:count])
    second = spreader(1, chips, rows, out_ref, full_out, *sems[count:])
    ticks, delay = rows - 1 + chips - 1, rows - 1
    _, total, padded, columns, channels = field_ref.shape
    band = padded - 2
    group = total // GROUPS

    def compute(index):
        at = index * group
        taps = [
            field_ref[b, pl.ds(at, group), a : a + band].reshape(group * band * columns, channels)
            for a in range(3)
            for b in range(3)
        ]
        window = jnp.concatenate(taps, axis=1)
        for part in range(2):
            weight = full_in[part]
            weight = weight.reshape(-1, weight.shape[-1])
            states = weight.shape[0]
            driven_ref[pl.ds(index * window.shape[0], window.shape[0]), part * states : (part + 1) * states] = (
                lax.dot_general(
                    window, weight, (((1,), (1,)), ((), ())), preferred_element_type=jnp.float32
                )
            )

    first[0]()
    for tick in range(ticks):
        first[1](tick)
        if tick == delay - 1:
            second[0]()
        if tick >= delay:
            second[1](tick - delay)
    first[3].wait()
    for index in range(GROUPS):
        compute(index)
        if ticks - delay + index < ticks:
            second[1](ticks - delay + index)
    for tick in range(ticks - delay + GROUPS, ticks):
        second[1](tick)
    first[2]()
    second[2]()
    second[3].wait()


def drive(own_in, own_out, field, chips, rows):
    many_in = own_in.shape[:1] + (rows,) + own_in.shape[1:]
    many_out = own_out.shape[:2] + (rows,) + own_out.shape[2:]
    _, total, padded, columns, channels = field.shape
    pixels = total * (padded - 2) * columns
    states = many_in[1] * many_in[2] * many_in[3] * many_in[4]
    vmem = pl.BlockSpec(memory_space=pltpu.VMEM)
    return pl.pallas_call(
        functools.partial(drive_kernel, chips, rows),
        out_shape=(
            jax.ShapeDtypeStruct((pixels, 2 * states), jnp.float32),
            jax.ShapeDtypeStruct(many_out, own_out.dtype),
        ),
        in_specs=[vmem, vmem, vmem],
        out_specs=(vmem, pl.BlockSpec(memory_space=pl.ANY)),
        scratch_shapes=[pltpu.VMEM(many_in, own_in.dtype)]
        + semaphores(chips, rows)
        + semaphores(chips, rows),
        compiler_params=pltpu.CompilerParams(
            collective_id=2, has_side_effects=True, vmem_limit_bytes=60 * 1024 * 1024
        ),
    )(own_in, own_out, field)


def spread(own, leads, chips, rows, number):
    shape = own.shape[: leads + 1] + (rows,) + own.shape[leads + 1 :]
    any_space = pl.BlockSpec(memory_space=pl.ANY)
    return pl.pallas_call(
        functools.partial(spread_kernel, leads, chips, rows),
        out_shape=jax.ShapeDtypeStruct(shape, own.dtype),
        in_specs=[pl.BlockSpec(memory_space=pltpu.VMEM)],
        out_specs=any_space,
        scratch_shapes=semaphores(chips, rows),
        compiler_params=pltpu.CompilerParams(collective_id=number, has_side_effects=True),
    )(own)


def conv(field, weight, form):
    return lax.conv_general_dilated(
        field, weight, (1, 1), ((0, 0), (1, 1)),
        dimension_numbers=("NHWC", form, "NHWC"),
        preferred_element_type=jnp.float32,
    )


def powers(log_rate, angle, exponent):
    modulus = jnp.exp(-log_rate * exponent)
    return modulus * jnp.cos(angle * exponent), modulus * jnp.sin(angle * exponent)


def on_device(frames_in, weight_in, weight_out, log_decay, rotation, start_state, skip_gain):
    frame_count, band_rows, columns, channels = frames_in.shape
    shard = weight_in.shape[1]
    chips, cores, rows = (lax.axis_size(a) for a in (CHIPS, CORE, ROWS))
    core, chip = lax.axis_index(CORE), lax.axis_index(CHIPS)
    half = shard // cores
    many = chips // 2
    piece = half // (2 * many)

    def own(vector, axis):
        picks = [
            jnp.concatenate(
                [
                    lax.slice_in_dim(vector, r * shard + c * half, r * shard + (c + 1) * half, axis=axis)
                    for r in range(rows)
                ],
                axis=axis,
            )
            for c in range(cores)
        ]
        return jnp.where(core == 0, picks[0], picks[1])

    states = rows * half
    slice_in = lax.dynamic_slice_in_dim(weight_in, core * half, half, 1)
    slice_out = lax.dynamic_slice_in_dim(weight_out, core * half, half, 2)
    own_in = slice_in.reshape(2, many, 2, piece, 9 * channels)
    own_out = slice_out.reshape(9, 2, many, 2, piece, channels)

    mine = with_halo(frames_in)
    theirs = swapped(mine)
    first = jnp.where(core == 0, mine, theirs)
    second = jnp.where(core == 0, theirs, mine)
    field = jnp.concatenate([first, second], axis=0)
    total = field.shape[0]

    if piece % 16 == 0 and total % GROUPS == 0:
        padded = jnp.pad(field, ((0, 0), (0, 0), (1, 1), (0, 0)))
        views = jnp.stack([padded[:, :, b : b + columns] for b in range(3)])
        both, out_full = drive(own_in, own_out, views, chips, rows)
        both = both.reshape(total, band_rows, columns, 2 * states)
        driven = [both[..., :states], both[..., states:]]
    else:
        in_full = spread(own_in, 0, chips, rows, 0).reshape(2, states, 3, 3, channels)
        out_full = spread(own_out, 1, chips, rows, 1)
        driven = [conv(field, in_full[part], "OHWI") for part in range(2)]

    log_rate, angle = own(log_decay, 0), own(rotation, 0)
    start = own(start_state, 3)
    lam_re, lam_im = powers(log_rate, angle, jnp.float32(1.0))
    state_re = jnp.where(chip == 0, start[:, :, 0], jnp.float32(0.0))
    state_im = jnp.where(chip == 0, start[:, :, 1], jnp.float32(0.0))
    local = []
    for t in range(total):
        state_re, state_im = (
            lam_re * state_re - lam_im * state_im + driven[0][t],
            lam_re * state_im + lam_im * state_re + driven[1][t],
        )
        local.append((state_re, state_im))
    tail = jnp.stack([state_re, state_im]).astype(jnp.bfloat16)
    carry_re = carry_im = jnp.float32(0.0)
    for step in range(1, chips):
        far = shifted(tail, CHIPS, step).astype(jnp.float32)
        jump_re, jump_im = powers(log_rate, angle, jnp.float32(total * (step - 1)))
        carry_re = carry_re + jump_re * far[0] - jump_im * far[1]
        carry_im = carry_im + jump_re * far[1] + jump_im * far[0]
    held = []
    for t in range(total):
        pow_re, pow_im = powers(log_rate, angle, jnp.float32(t + 1))
        held.append(
            jnp.concatenate(
                [
                    local[t][0] + pow_re * carry_re - pow_im * carry_im,
                    local[t][1] + pow_re * carry_im + pow_im * carry_re,
                ],
                axis=-1,
            ).astype(jnp.bfloat16)
        )
    held = with_halo(jnp.stack(held))

    out_weight = out_full.reshape(3, 3, 2 * states, channels)
    held_theirs = lax.dynamic_slice_in_dim(held, (1 - core) * frame_count, frame_count, 0)
    held_mine = lax.dynamic_slice_in_dim(held, core * frame_count, frame_count, 0)
    sent = conv(held_theirs, out_weight, "HWIO").astype(jnp.bfloat16)
    got = swapped(sent).astype(jnp.float32)
    mixing = conv(held_mine, out_weight, "HWIO") + got
    pre_act = mixing + skip_gain * frames_in.astype(jnp.float32)
    return jax.nn.gelu(pre_act, approximate=False).astype(jnp.bfloat16)


def solution(mesh):
    count, rows = mesh.devices.shape
    fine = Mesh(mesh.devices.reshape(count // 2, 2, rows), (CHIPS, CORE, ROWS))
    frames = P((CHIPS, CORE), ROWS, None, None)
    return jax.shard_map(
        on_device,
        mesh=fine,
        in_specs=(
            frames,
            P(None, ROWS, None),
            P(None, None, ROWS, None),
            P(),
            P(),
            P(ROWS, None, None, None),
            P(),
        ),
        out_specs=frames,
        check_vma=False,
    )
```

```python
import functools
import jax
import jax.numpy as jnp
from jax import lax
from jax.experimental import pallas as pl
from jax.experimental.pallas import tpu as pltpu
from jax.sharding import Mesh, PartitionSpec as P

CHIPS, CORE, ROWS = "chips", "core", "rows"


def shifted(value, axis, step):
    count = lax.axis_size(axis)
    pairs = [(i, i + step) for i in range(count) if 0 <= i + step < count]
    return lax.ppermute(value, axis, pairs)


def swapped(value):
    return lax.ppermute(value, CORE, [(0, 1), (1, 0)])


def with_halo(field):
    above = shifted(field[:, -1:], ROWS, 1)
    below = shifted(field[:, :1], ROWS, -1)
    return jnp.concatenate([above, field, below], axis=1)


def chip_at(place, chips):
    far = place // (chips // 2)
    return (1 - far) * (2 * place) + far * (2 * (chips - 1 - place) + 1)


def place_of(chip, chips):
    odd = chip % 2
    return (1 - odd) * (chip // 2) + odd * (chips - 1 - chip // 2)


def meet(chips, rows, chip, row, onward, back):
    barrier = pltpu.get_barrier_semaphore()

    def greet(**where):
        pl.semaphore_signal(
            barrier, inc=1, device_id=where, device_id_type=pl.DeviceIdType.MESH
        )

    greet(chips=onward)
    greet(chips=back)

    @pl.when(row > 0)
    def _():
        greet(rows=row - 1)

    @pl.when(row < rows - 1)
    def _():
        greet(rows=row + 1)

    sides = (row + rows - 1) // rows + (2 * rows - 2 - row) // rows
    pl.semaphore_wait(barrier, 2 + sides)


def spreader(leads, chips, rows, own_ref, full_ref, z_send, z_recv, r_send, r_recv, own_sem):
    chip, row = lax.axis_index(CHIPS), lax.axis_index(ROWS)
    place = place_of(chip, chips)
    onward = chip_at((place + 1) % chips, chips)
    back = chip_at((place + chips - 1) % chips, chips)
    many = chips // 2
    lead = (slice(None),) * leads

    def own_slice():
        return own_ref.at[lead + (chip // many, chip % many)]

    def block(shard, source, piece=None):
        at = lead + (source // many, shard, source % many)
        return full_ref.at[at if piece is None else at + (piece,)]

    keep = pltpu.make_async_copy(
        own_ref, full_ref.at[lead + (slice(None), row)], own_sem
    )

    def line(side, step):
        step_way = 1 - 2 * side
        shard = row - step_way * step
        src = own_slice() if step == 0 else block(shard, chip)
        return pltpu.make_async_remote_copy(
            src_ref=src,
            dst_ref=block(shard, chip),
            send_sem=z_send.at[side, step],
            recv_sem=z_recv.at[side, step],
            device_id={ROWS: row + step_way},
            device_id_type=pl.DeviceIdType.MESH,
        )

    def landed(side, step):
        shard = row - (1 - 2 * side) * (step + 1)
        here = block(shard, chip)
        return pltpu.make_async_remote_copy(
            src_ref=here,
            dst_ref=here,
            send_sem=z_send.at[side, step],
            recv_sem=z_recv.at[side, step],
            device_id={ROWS: row},
            device_id_type=pl.DeviceIdType.MESH,
        )

    def ring(side, step, way, turn):
        turn_way = 1 - 2 * way
        shard = row - (1 - 2 * side) * (step + 1)
        source = chip_at((place - turn_way * turn + chips) % chips, chips)
        here = block(shard, source, way)
        return pltpu.make_async_remote_copy(
            src_ref=here,
            dst_ref=here,
            send_sem=r_send.at[side, step, way, turn],
            recv_sem=r_recv.at[side, step, way, turn],
            device_id={CHIPS: back if way else onward},
            device_id_type=pl.DeviceIdType.MESH,
        )

    def ring_landed(side, step, way, turn):
        turn_way = 1 - 2 * way
        shard = row - (1 - 2 * side) * (step + 1)
        source = chip_at((place - turn_way * (turn + 1) + 2 * chips) % chips, chips)
        here = block(shard, source, way)
        return pltpu.make_async_remote_copy(
            src_ref=here,
            dst_ref=here,
            send_sem=r_send.at[side, step, way, turn],
            recv_sem=r_recv.at[side, step, way, turn],
            device_id={CHIPS: back if way else onward},
            device_id_type=pl.DeviceIdType.MESH,
        )

    def sends(side, step):
        near = row - step if side == 0 else rows - 1 - row - step
        room = rows - 1 - row if side == 0 else row
        return jnp.logical_and(near >= 0, room > 0)

    def comes(side, step):
        return (row if side == 0 else rows - 1 - row) > step

    def begin():
        keep.start()
        for side in range(2):

            @pl.when(sends(side, 0))
            def _():
                line(side, 0).start()

    def advance(tick):
        if tick < rows - 1:
            for side in range(2):

                @pl.when(comes(side, tick))
                def _():
                    landed(side, tick).wait_recv()
                    if tick + 1 < rows - 1:

                        @pl.when(sends(side, tick + 1))
                        def _():
                            line(side, tick + 1).start()

                    for way in range(2):
                        ring(side, tick, way, 0).start()

        for turn in range(1, chips):
            step = tick - turn
            if 0 <= step < rows - 1:
                for side in range(2):

                    @pl.when(comes(side, step))
                    def _():
                        for way in range(2):
                            ring_landed(side, step, way, turn - 1).wait_recv()
                            if turn < chips - 1:
                                ring(side, step, way, turn).start()

    def finish():
        for side in range(2):
            for step in range(rows - 1):

                @pl.when(sends(side, step))
                def _():
                    line(side, step).wait_send()

                @pl.when(comes(side, step))
                def _():
                    for way in range(2):
                        for turn in range(chips - 1):
                            ring(side, step, way, turn).wait_send()

    return begin, advance, finish, keep


def spread_kernel(leads, chips, rows, *refs):
    chip, row = lax.axis_index(CHIPS), lax.axis_index(ROWS)
    place = place_of(chip, chips)
    onward = chip_at((place + 1) % chips, chips)
    back = chip_at((place + chips - 1) % chips, chips)
    meet(chips, rows, chip, row, onward, back)
    begin, advance, finish, keep = spreader(leads, chips, rows, *refs)
    begin()
    for tick in range(rows - 1 + chips - 1):
        advance(tick)
    finish()
    keep.wait()


def semaphores(chips, rows):
    return [
        pltpu.SemaphoreType.DMA((2, rows - 1)),
        pltpu.SemaphoreType.DMA((2, rows - 1)),
        pltpu.SemaphoreType.DMA((2, rows - 1, 2, chips - 1)),
        pltpu.SemaphoreType.DMA((2, rows - 1, 2, chips - 1)),
        pltpu.SemaphoreType.DMA,
    ]


GROUPS = 4


def drive_kernel(chips, rows, in_ref, out_ref, field_ref, driven_ref, full_out, full_in, views, *sems):
    chip, row = lax.axis_index(CHIPS), lax.axis_index(ROWS)
    place = place_of(chip, chips)
    onward = chip_at((place + 1) % chips, chips)
    back = chip_at((place + chips - 1) % chips, chips)
    meet(chips, rows, chip, row, onward, back)
    count = len(sems) // 2
    first = spreader(0, chips, rows, in_ref, full_in, *sems[:count])
    second = spreader(1, chips, rows, out_ref, full_out, *sems[count:])
    ticks, delay = rows - 1 + chips - 1, rows - 1
    total, padded, columns, channels = field_ref.shape
    band = padded - 2
    group = total // GROUPS

    def compute(index):
        at = index * group
        taps = [
            views[b, at : at + group, a : a + band].reshape(group * band * columns, channels)
            for a in range(3)
            for b in range(3)
        ]
        window = jnp.concatenate(taps, axis=1)
        for part in range(2):
            weight = full_in[part]
            weight = weight.reshape(-1, weight.shape[-1])
            states = weight.shape[0]
            driven_ref[pl.ds(index * window.shape[0], window.shape[0]), part * states : (part + 1) * states] = (
                lax.dot_general(
                    window, weight, (((1,), (1,)), ((), ())), preferred_element_type=jnp.float32
                )
            )

    first[0]()

    @pl.loop(0, total)
    def _(frame):
        whole = field_ref[frame]
        wide = whole.astype(jnp.float32)
        edge = jnp.zeros((padded, 1, channels), jnp.float32)
        before = jnp.concatenate([edge, wide[:, : columns - 1]], axis=1)
        after = jnp.concatenate([wide[:, 1:], edge], axis=1)
        views[0, frame] = before.astype(whole.dtype)
        views[1, frame] = whole
        views[2, frame] = after.astype(whole.dtype)

    for tick in range(ticks):
        first[1](tick)
        if tick == delay - 1:
            second[0]()
        if tick >= delay:
            second[1](tick - delay)
    first[3].wait()
    for index in range(GROUPS):
        compute(index)
        if ticks - delay + index < ticks:
            second[1](ticks - delay + index)
    for tick in range(ticks - delay + GROUPS, ticks):
        second[1](tick)
    first[2]()
    second[2]()
    second[3].wait()


def drive(own_in, own_out, field, chips, rows):
    many_in = own_in.shape[:1] + (rows,) + own_in.shape[1:]
    many_out = own_out.shape[:2] + (rows,) + own_out.shape[2:]
    total, padded, columns, channels = field.shape
    pixels = total * (padded - 2) * columns
    states = many_in[1] * many_in[2] * many_in[3] * many_in[4]
    vmem = pl.BlockSpec(memory_space=pltpu.VMEM)
    return pl.pallas_call(
        functools.partial(drive_kernel, chips, rows),
        out_shape=(
            jax.ShapeDtypeStruct((pixels, 2 * states), jnp.float32),
            jax.ShapeDtypeStruct(many_out, own_out.dtype),
        ),
        in_specs=[vmem, vmem, vmem],
        out_specs=(vmem, pl.BlockSpec(memory_space=pl.ANY)),
        scratch_shapes=[
            pltpu.VMEM(many_in, own_in.dtype),
            pltpu.VMEM((3,) + field.shape, field.dtype),
        ]
        + semaphores(chips, rows)
        + semaphores(chips, rows),
        compiler_params=pltpu.CompilerParams(
            collective_id=2, has_side_effects=True, vmem_limit_bytes=60 * 1024 * 1024
        ),
    )(own_in, own_out, field)


def spread(own, leads, chips, rows, number):
    shape = own.shape[: leads + 1] + (rows,) + own.shape[leads + 1 :]
    any_space = pl.BlockSpec(memory_space=pl.ANY)
    return pl.pallas_call(
        functools.partial(spread_kernel, leads, chips, rows),
        out_shape=jax.ShapeDtypeStruct(shape, own.dtype),
        in_specs=[pl.BlockSpec(memory_space=pltpu.VMEM)],
        out_specs=any_space,
        scratch_shapes=semaphores(chips, rows),
        compiler_params=pltpu.CompilerParams(collective_id=number, has_side_effects=True),
    )(own)


def conv(field, weight, form):
    return lax.conv_general_dilated(
        field, weight, (1, 1), ((0, 0), (1, 1)),
        dimension_numbers=("NHWC", form, "NHWC"),
        preferred_element_type=jnp.float32,
    )


def recur_kernel(last_only, both_ref, begin_ref, factor_ref, result_ref):
    states = factor_ref.shape[1]
    lam_re, lam_im = factor_ref[0:1, :], factor_ref[1:2, :]
    state_re, state_im = begin_ref[0, :, :states], begin_ref[0, :, states:]
    total = both_ref.shape[0]
    for t in range(total):
        state_re, state_im = (
            lam_re * state_re - lam_im * state_im + both_ref[t, 0, :, :states],
            lam_re * state_im + lam_im * state_re + both_ref[t, 0, :, states:],
        )
        if not last_only:
            result_ref[t, 0, :, :states] = state_re.astype(result_ref.dtype)
            result_ref[t, 0, :, states:] = state_im.astype(result_ref.dtype)
    if last_only:
        result_ref[0, :, :states] = state_re.astype(result_ref.dtype)
        result_ref[0, :, states:] = state_im.astype(result_ref.dtype)


def recur(both, begin, factor, last_only):
    total, band, columns, lanes = both.shape
    frames = pl.BlockSpec((total, 1, columns, lanes), lambda i: (0, i, 0, 0))
    single = pl.BlockSpec((1, columns, lanes), lambda i: (i, 0, 0))
    shape = both.shape[1:] if last_only else both.shape
    return pl.pallas_call(
        functools.partial(recur_kernel, last_only),
        out_shape=jax.ShapeDtypeStruct(shape, jnp.bfloat16),
        grid=(band,),
        in_specs=[frames, single, pl.BlockSpec(factor.shape, lambda i: (0, 0))],
        out_specs=single if last_only else frames,
    )(both, begin, factor)


def powers(log_rate, angle, exponent):
    modulus = jnp.exp(-log_rate * exponent)
    return modulus * jnp.cos(angle * exponent), modulus * jnp.sin(angle * exponent)


def on_device(frames_in, weight_in, weight_out, log_decay, rotation, start_state, skip_gain):
    frame_count, band_rows, columns, channels = frames_in.shape
    shard = weight_in.shape[1]
    chips, cores, rows = (lax.axis_size(a) for a in (CHIPS, CORE, ROWS))
    core, chip = lax.axis_index(CORE), lax.axis_index(CHIPS)
    half = shard // cores
    many = chips // 2
    piece = half // (2 * many)

    def own(vector, axis):
        picks = [
            jnp.concatenate(
                [
                    lax.slice_in_dim(vector, r * shard + c * half, r * shard + (c + 1) * half, axis=axis)
                    for r in range(rows)
                ],
                axis=axis,
            )
            for c in range(cores)
        ]
        return jnp.where(core == 0, picks[0], picks[1])

    states = rows * half
    slice_in = lax.dynamic_slice_in_dim(weight_in, core * half, half, 1)
    slice_out = lax.dynamic_slice_in_dim(weight_out, core * half, half, 2)
    own_in = slice_in.reshape(2, many, 2, piece, 9 * channels)
    own_out = slice_out.reshape(9, 2, many, 2, piece, channels)

    mine = with_halo(frames_in)
    theirs = swapped(mine)
    first = jnp.where(core == 0, mine, theirs)
    second = jnp.where(core == 0, theirs, mine)
    field = jnp.concatenate([first, second], axis=0)
    total = field.shape[0]

    if piece % 16 == 0 and total % GROUPS == 0:
        both, out_full = drive(own_in, own_out, field, chips, rows)
        both = both.reshape(total, band_rows, columns, 2 * states)
    else:
        in_full = spread(own_in, 0, chips, rows, 0).reshape(2, states, 3, 3, channels)
        out_full = spread(own_out, 1, chips, rows, 1)
        both = jnp.concatenate(
            [conv(field, in_full[part], "OHWI") for part in range(2)], axis=-1
        )

    log_rate, angle = own(log_decay, 0), own(rotation, 0)
    start = own(start_state, 3)
    lam_re, lam_im = powers(log_rate, angle, jnp.float32(1.0))
    begin = jnp.concatenate([start[:, :, 0], start[:, :, 1]], axis=-1)
    begin = jnp.where(chip == 0, begin, jnp.float32(0.0))
    factor = jnp.stack([lam_re, lam_im])
    tail = recur(both, begin, factor, True)
    carry_re = carry_im = jnp.float32(0.0)
    for step in range(1, chips):
        far = shifted(tail, CHIPS, step).astype(jnp.float32)
        jump_re, jump_im = powers(log_rate, angle, jnp.float32(total * (step - 1)))
        carry_re = carry_re + jump_re * far[..., :states] - jump_im * far[..., states:]
        carry_im = carry_im + jump_re * far[..., states:] + jump_im * far[..., :states]
    begin = begin + jnp.concatenate([carry_re, carry_im], axis=-1)
    held = with_halo(recur(both, begin, factor, False))

    out_weight = out_full.reshape(3, 3, 2 * states, channels)
    held_theirs = lax.dynamic_slice_in_dim(held, (1 - core) * frame_count, frame_count, 0)
    held_mine = lax.dynamic_slice_in_dim(held, core * frame_count, frame_count, 0)
    sent = conv(held_theirs, out_weight, "HWIO").astype(jnp.bfloat16)
    got = swapped(sent).astype(jnp.float32)
    mixing = conv(held_mine, out_weight, "HWIO") + got
    pre_act = mixing + skip_gain * frames_in.astype(jnp.float32)
    return jax.nn.gelu(pre_act, approximate=False).astype(jnp.bfloat16)


def solution(mesh):
    count, rows = mesh.devices.shape
    fine = Mesh(mesh.devices.reshape(count // 2, 2, rows), (CHIPS, CORE, ROWS))
    frames = P((CHIPS, CORE), ROWS, None, None)
    return jax.shard_map(
        on_device,
        mesh=fine,
        in_specs=(
            frames,
            P(None, ROWS, None),
            P(None, None, ROWS, None),
            P(),
            P(),
            P(ROWS, None, None, None),
            P(),
        ),
        out_specs=frames,
        check_vma=False,
    )
```
